32 devices in a mesh: dp: 8 (over z, x), tensor: 4 (over y, core).
Axes of the slice: x: 2, y: 2, z: 4, core: 2. Of those that a mesh axis runs over, the one named last changes fastest.
Arguments:
- tokens: bfloat16 [1024, 8192], P('dp', 'tensor'), may hold values from -6 to 6
- key_value_weight: bfloat16 [8192, 2048], P('tensor'), may hold values from -0.0625 to 0.0625
- adapter_down_weight: bfloat16 [24, 64, 8192], P('dp', None, 'tensor'), may hold values from -0.0625 to 0.0625
- adapter_up_weight: bfloat16 [24, 64, 2048], P('dp', None, 'tensor'), may hold values from -0.75 to 0.75
- cotangent: bfloat16 [1024, 2048], P('dp', 'tensor'), may hold values from -3 to 3
- sequence_adapter_index: int32 [32], replicated, may hold values from 0 to 23, as said below
- adapter_storage_row: int32 [24], replicated, may hold values from 0 to 23, as said below
Outputs:
- key_value_output: bfloat16 [1024, 2048], P('dp', 'tensor')
- token_gradient: bfloat16 [1024, 8192], P('dp', 'tensor')
- grad_down: float32 [24, 64, 8192], P('dp', None, 'tensor')
- grad_up: float32 [24, 64, 2048], P('dp', None, 'tensor')
The draws below stay inside these ranges and needn't reach their ends.
Inputs may be any that keep to these rules, and one draw needn't show every extreme that they name: Each value appears once: adapter a is held at row adapter_storage_row[a] of adapter_down_weight, adapter_up_weight, grad_down and grad_up, on index adapter_storage_row[a] // 3 of dp. `sequence_adapter_index`: the 4 sequences i that share one value of i // 4 use adapters held on 4 different indices of dp.
All inputs are finite; a program needn't handle non-finite values.
Results may differ from the reference program's by a relative error of at most 0.02.
Values may be sent and summed in bfloat16 or wider, within the bound.
A program may use at most 64 MiB of HBM per device.

```python
import jax
import jax.numpy as jnp
from jax import lax

MODEL_WIDTH = 8192
ADAPTER_RANK = 64
SEQS_DEV = 4
ADP_DEV = 3
KEY_VALUE_WIDTH = 2048
TOKENS = 1024
ADAPTER_TOTAL = 24
N_DP = 8
N_TENSOR = 4


def adapter_tables(key):
    base_key = jax.random.fold_in(key, 11)
    storage = jax.random.permutation(jax.random.fold_in(base_key, 1), ADP_DEV * N_DP).astype(jnp.int32)
    reader_keys = jax.random.split(jax.random.fold_in(base_key, 2), N_DP)

    def owners_for(reader_key):
        return jax.random.permutation(reader_key, N_DP)[:SEQS_DEV]
    owners = jax.vmap(owners_for)(reader_keys).astype(jnp.int32)
    draw_one = jax.random.randint(jax.random.fold_in(base_key, 3), (N_DP, SEQS_DEV), 0, ADP_DEV)
    draw_two = jax.random.randint(jax.random.fold_in(base_key, 4), (N_DP, SEQS_DEV), 0, ADP_DEV)
    within = jnp.minimum(draw_one, draw_two).astype(jnp.int32)
    held_rows = (owners * ADP_DEV + within).reshape(-1)
    inverse = jnp.argsort(storage).astype(jnp.int32)
    chosen = inverse[held_rows]
    return (storage, chosen.astype(jnp.int32))


def draw_adapter_storage_row(key, part):
    return adapter_tables(key)[0]


def draw_sequence_adapter_index(key, part):
    return adapter_tables(key)[1]


def block_levels(stream_key, shape, cuts, low, top_value):
    factor_of = 1.0
    for axis_at, shards_of in cuts:
        draws = jax.random.uniform(jax.random.fold_in(jax.random.fold_in(stream_key, 6), axis_at), (shards_of,), jnp.float32, low / len(cuts), top_value / len(cuts))
        factor_of = factor_of * jnp.repeat(jnp.exp(draws), shape[axis_at] // shards_of).reshape((-1,) + (1,) * (len(shape) - 1 - axis_at))
    return factor_of


def scatter_about(rng, dims, deviation, bound, cuts=(), held_as=jnp.bfloat16):
    factor_of = block_levels(rng, dims, cuts, -0.22, 0.18) if cuts else 1.0
    array = jax.random.normal(rng, dims, jnp.float32) * deviation * factor_of
    return jnp.minimum(jnp.maximum(array, -bound), bound).astype(held_as)


def setup_inputs(seed: int = 0) -> dict:
    keys = jax.random.split(jax.random.key(seed), 8)
    return {
        "tokens": scatter_about(keys[0], (TOKENS, MODEL_WIDTH), 1.0, 6.0, ((0, 8), (1, 4))),
        "key_value_weight": scatter_about(keys[1], (MODEL_WIDTH, KEY_VALUE_WIDTH), MODEL_WIDTH ** -0.5, 0.0625, ((0, 4),)),
        "adapter_down_weight": scatter_about(keys[2], (ADAPTER_TOTAL, ADAPTER_RANK, MODEL_WIDTH), MODEL_WIDTH ** -0.5, 0.0625, ((0, 8), (2, 4))),
        "adapter_up_weight": scatter_about(keys[3], (ADAPTER_TOTAL, ADAPTER_RANK, KEY_VALUE_WIDTH), ADAPTER_RANK ** -0.5, 0.75, ((0, 8), (2, 4))),
        "cotangent": scatter_about(keys[4], (TOKENS, KEY_VALUE_WIDTH), 0.5, 3.0, ((0, 8), (1, 4))),
        "sequence_adapter_index": draw_sequence_adapter_index(jax.random.fold_in(keys[7], 71), 0),
        "adapter_storage_row": draw_adapter_storage_row(jax.random.fold_in(keys[7], 71), 0),
    }


adapter_scale = 0.25


def reference(tokens, key_value_weight, adapter_down_weight, adapter_up_weight, cotangent, sequence_adapter_index, adapter_storage_row):
    adapters = adapter_storage_row.shape[0]
    seq_total = sequence_adapter_index.shape[0]
    adapter_codes = jnp.arange(adapters, dtype=jnp.int32)
    matches = sequence_adapter_index[:, None] == adapter_codes[None, :]
    seq_rows = jnp.sum(jnp.where(matches, adapter_storage_row[None, :], 0), axis=1).astype(jnp.int32)
    row_hits = seq_rows[:, None] == adapter_codes[None, :]
    usage_count = jnp.sum(row_hits.astype(jnp.float32), axis=0)
    inverse_use = 1.0 / jnp.maximum(usage_count, 1.0)
    feature_width = tokens.shape[1]
    seq_length = tokens.shape[0] // seq_total
    block_span = feature_width // N_TENSOR
    out_width = key_value_weight.shape[1]
    weight_blocks = key_value_weight.reshape(N_TENSOR, block_span, out_width).astype(jnp.float32)
    weight_turned = key_value_weight.T
    token_sequences = tokens.reshape(seq_total, seq_length, feature_width)
    cot_seqs = cotangent.reshape(seq_total, seq_length, out_width)

    def one_sequence(totals, inputs):
        grad_down, grad_up = totals
        sequence_tokens, sequence_cotangent, sequence_row = inputs
        down_matrix_rows = lax.dynamic_index_in_dim(adapter_down_weight, sequence_row, 0, keepdims=False)
        up_matrix_rows = lax.dynamic_index_in_dim(adapter_up_weight, sequence_row, 0, keepdims=False)
        pieces = sequence_tokens.reshape(seq_length, N_TENSOR, block_span).astype(jnp.float32)
        partial_value = jnp.einsum("lnd,ndo->nlo", pieces, weight_blocks)
        partial_round = lax.optimization_barrier(partial_value.astype(jnp.bfloat16)).astype(jnp.float32)
        frozen_backbone = jnp.sum(partial_round, axis=0)
        inner_full = jnp.dot(sequence_tokens, down_matrix_rows.T, preferred_element_type=jnp.float32)
        middle_round = inner_full.astype(jnp.bfloat16)
        back_full = jnp.dot(sequence_cotangent, up_matrix_rows.T, preferred_element_type=jnp.float32)
        backward_round = back_full.astype(jnp.bfloat16)
        output_list = (frozen_backbone + adapter_scale * jnp.dot(middle_round, up_matrix_rows, preferred_element_type=jnp.float32)).astype(jnp.bfloat16)
        grad_in = (jnp.dot(sequence_cotangent, weight_turned, preferred_element_type=jnp.float32)
                   + adapter_scale * jnp.dot(backward_round, down_matrix_rows, preferred_element_type=jnp.float32)).astype(jnp.bfloat16)
        down_term = (adapter_scale * jnp.dot(backward_round.T, sequence_tokens, preferred_element_type=jnp.float32)).astype(jnp.bfloat16)
        up_term = (adapter_scale * jnp.dot(middle_round.T, sequence_cotangent, preferred_element_type=jnp.float32)).astype(jnp.bfloat16)
        grad_down = grad_down.at[sequence_row].add(down_term.astype(jnp.float32))
        grad_up = grad_up.at[sequence_row].add(up_term.astype(jnp.float32))
        return (grad_down, grad_up), (output_list, grad_in)

    down_start_offset = jnp.zeros(adapter_down_weight.shape, jnp.float32)
    up_start_offset = jnp.zeros(adapter_up_weight.shape, jnp.float32)
    (grad_down, grad_up), (output_list, grad_in) = lax.scan(one_sequence, (down_start_offset, up_start_offset), (token_sequences, cot_seqs, seq_rows))
    key_value_output = output_list.reshape(seq_total * seq_length, out_width)
    token_gradient = grad_in.reshape(seq_total * seq_length, feature_width)
    grad_down = grad_down * inverse_use[:, None, None]
    grad_up = grad_up * inverse_use[:, None, None]
    return (key_value_output, token_gradient, grad_down, grad_up)
```

```python
import functools

import jax
import jax.numpy as jnp
from jax import lax
from jax.experimental import pallas as pl
from jax.experimental.pallas import tpu as pltpu
from jax.sharding import PartitionSpec as P

adapter_scale = 0.25
MESH = pl.DeviceIdType.MESH
F32 = jnp.float32
BF16 = jnp.bfloat16


def nt_dot(a, b):
    return lax.dot_general(a, b, (((1,), (1,)), ((), ())), preferred_element_type=F32)


def tn_dot(a, b):
    return lax.dot_general(a, b, (((0,), (0,)), ((), ())), preferred_element_type=F32)


def routes(dp_count, seqs, resident, seq_ref, store_ref, table_ref, weight_ref):
    d = lax.axis_index("dp")
    rows = [store_ref[seq_ref[d * seqs + j]] for j in range(seqs)]
    dist = [lax.rem(lax.div(r, jnp.int32(resident)) + dp_count - d, dp_count) for r in rows]
    for j in range(seqs):
        table_ref[2 * dp_count + j] = dist[j]
    for k in range(dp_count):
        pick = jnp.int32(0)
        for j in range(seqs):
            pick = jnp.where(dist[j] == k, jnp.int32(j), pick)
        table_ref[k] = pick
    counts = [jnp.float32(0.0)] * resident
    for k in range(dp_count):
        reader = lax.rem(d + dp_count - k, dp_count)
        found = jnp.int32(-1)
        for j in range(seqs):
            local = store_ref[seq_ref[reader * seqs + j]] - d * resident
            found = jnp.where((local >= 0) & (local < resident), local, found)
        table_ref[dp_count + k] = jnp.maximum(found, 0)
        for a in range(resident):
            hit = jnp.where(found == a, jnp.float32(1.0), jnp.float32(0.0))
            weight_ref[a * dp_count + k] = hit
            counts[a] = counts[a] + hit
    for a in range(resident):
        weight_ref[resident * dp_count + a] = counts[a]


def kernel(
    dp_count,
    tensor_count,
    groups,
    table_ref,
    weight_ref,
    tok_ref,
    w_ref,
    down_ref,
    up_ref,
    cot_ref,
    cot_seq_ref,
    kvo_ref,
    tg_ref,
    gd_ref,
    gu_ref,
    w_v,
    slot_out,
    slot_in,
    ret_out,
    ret_in,
    cots,
    parts,
    part_in,
    ranks,
    back_m,
    inner_m,
    acc,
    w_sem,
    slot_ssem,
    slot_rsem,
    ret_ssem,
    ret_rsem,
    cot_ssem,
    cot_rsem,
    part_ssem,
    part_rsem,
    rank_ssem,
    rank_rsem,
):
    d = lax.axis_index("dp")
    t = lax.axis_index("tensor")
    resident, rank, block = down_ref.shape
    out_block = up_ref.shape[2]
    seqs, length = tok_ref.shape[:2]
    rows = seqs * length
    per_group = dp_count // groups

    def dp_to(k):
        return lax.rem(d + k, dp_count)

    def dp_from(k):
        return lax.rem(d + dp_count - k, dp_count)

    def t_to(q):
        return lax.rem(t + q, tensor_count)

    def t_from(q):
        return lax.rem(t + tensor_count - q, tensor_count)

    def w_copy(i):
        c = t_to(i)
        return pltpu.make_async_copy(
            w_ref.at[:, pl.ds(pl.multiple_of(c * out_block, out_block), out_block)],
            w_v.at[i],
            w_sem.at[i],
        )

    for i in range(tensor_count):
        w_copy(i).start()

    barrier = pltpu.get_barrier_semaphore()
    for k in range(1, dp_count):
        pl.semaphore_signal(barrier, inc=1, device_id={"dp": dp_to(k)}, device_id_type=MESH)
    for q in range(1, tensor_count):
        pl.semaphore_signal(barrier, inc=1, device_id={"tensor": t_to(q)}, device_id_type=MESH)

    for k in range(dp_count):
        pick = table_ref[k]
        target = slot_in if k == 0 else slot_out
        target[k * length:(k + 1) * length, :block] = tok_ref[pick]
        target[k * length:(k + 1) * length, block:] = cot_seq_ref[pick]

    pl.semaphore_wait(barrier, dp_count + tensor_count - 2)

    def cot_copy(q):
        return pltpu.make_async_remote_copy(
            cot_ref, cots.at[q], cot_ssem.at[q], cot_rsem.at[q],
            device_id={"tensor": t_to(q)}, device_id_type=MESH)

    def slot_copy(k):
        at = pl.ds(k * length, length)
        return pltpu.make_async_remote_copy(
            slot_out.at[at], slot_in.at[at], slot_ssem.at[k], slot_rsem.at[k],
            device_id={"dp": dp_to(k)}, device_id_type=MESH)

    def ret_copy(k):
        return pltpu.make_async_remote_copy(
            ret_out.at[k], ret_in.at[k], ret_ssem.at[k], ret_rsem.at[k],
            device_id={"dp": dp_from(k)}, device_id_type=MESH)

    def part_copy(q):
        return pltpu.make_async_remote_copy(
            parts.at[q], part_in.at[q], part_ssem.at[q], part_rsem.at[q],
            device_id={"tensor": t_to(q)}, device_id_type=MESH)

    def rank_copy(g, q):
        return pltpu.make_async_remote_copy(
            ranks.at[g, t], ranks.at[g, t], rank_ssem.at[g, q], rank_rsem.at[g, q],
            device_id={"tensor": t_to(q)}, device_id_type=MESH)

    for k in range(1, dp_count):
        slot_copy(k).start()
    for q in range(1, tensor_count):
        cot_copy(q).start()

    adapter_of = [table_ref[dp_count + k] for k in range(dp_count)]
    weights = [[weight_ref[a * dp_count + k] for k in range(dp_count)] for a in range(resident)]
    counts = [weight_ref[resident * dp_count + a] for a in range(resident)]

    def frozen_block(i, carry):
        w_copy(i).wait()
        parts[i] = jnp.dot(tok_ref[...].reshape(rows, block), w_v[i], preferred_element_type=F32).astype(BF16)
        return carry

    lax.fori_loop(0, tensor_count, frozen_block, 0)

    def rank_stage(g):
        for m in range(per_group):
            k = g * per_group + m
            if k:
                slot_copy(k).wait_recv()
            x = slot_in[k * length:(k + 1) * length, :block]
            c = slot_in[k * length:(k + 1) * length, block:]
            inner = nt_dot(x, down_ref[adapter_of[k]])
            back = nt_dot(c, up_ref[adapter_of[k]])
            ranks[g, t, m * length:(m + 1) * length, :] = jnp.concatenate(
                [inner, back], axis=1).astype(BF16)
        for q in range(1, tensor_count):
            rank_copy(g, q).start()

    def base_block(i, carry):
        q = lax.rem(tensor_count - i, tensor_count)
        acc[...] += nt_dot(cots[q], w_v[i])
        return carry

    def use_stage(g):
        for q in range(1, tensor_count):
            s = t_from(q)
            pltpu.make_async_remote_copy(
                ranks.at[g, s], ranks.at[g, s], rank_ssem.at[g, q], rank_rsem.at[g, q],
                device_id={"tensor": t_to(q)}, device_id_type=MESH).wait_recv()
        for q in range(1, tensor_count):
            rank_copy(g, q).wait_send()
        total = ranks[g, 0].astype(F32)
        for s in range(1, tensor_count):
            total = total + ranks[g, s].astype(F32)
        for m in range(per_group):
            k = g * per_group + m
            lines = total[m * length:(m + 1) * length]
            inner = lines[:, :rank].astype(BF16)
            back = lines[:, rank:].astype(BF16)
            target = ret_out if k else ret_in
            target[k, :, :block] = (adapter_scale * jnp.dot(
                back, down_ref[adapter_of[k]], preferred_element_type=F32)).astype(BF16)
            target[k, :, block:] = (adapter_scale * jnp.dot(
                inner, up_ref[adapter_of[k]], preferred_element_type=F32)).astype(BF16)
            for a in range(resident):
                at = slice(k * length, (k + 1) * length)
                back_m[a, at, :] = (back.astype(F32) * weights[a][k]).astype(BF16)
                inner_m[a, at, :] = (inner.astype(F32) * weights[a][k]).astype(BF16)
            if k:
                ret_copy(k).start()

    rank_stage(0)
    for q in range(1, tensor_count):
        part_copy(q).start()
    acc[...] = nt_dot(cot_ref[...], w_v[0])
    for q in range(1, tensor_count):
        cot_copy(q).wait_recv()
    half = max(1, tensor_count // 2)
    lax.fori_loop(1, half, base_block, 0)
    use_stage(0)
    for g in range(1, groups):
        rank_stage(g)
        if g == 1:
            lax.fori_loop(half, tensor_count, base_block, 0)
        use_stage(g)

    x_all = slot_in[:, :block]
    c_all = slot_in[:, block:]
    for a in range(resident):
        gd_ref[a] = tn_dot(back_m[a], x_all) * (
            adapter_scale / jnp.maximum(jnp.full((1, block), counts[a], F32), 1.0))
        gu_ref[a] = tn_dot(inner_m[a], c_all) * (
            adapter_scale / jnp.maximum(jnp.full((1, out_block), counts[a], F32), 1.0))

    for q in range(1, tensor_count):
        part_copy(q).wait_recv()
    backbone = parts[0].astype(F32)
    for q in range(1, tensor_count):
        backbone = backbone + part_in[q].astype(F32)
    for k in range(1, dp_count):
        ret_copy(k).wait_recv()
    for j in range(seqs):
        at = slice(j * length, (j + 1) * length)
        came = ret_in[table_ref[2 * dp_count + j]]
        kvo_ref[at, :] = (backbone[at] + came[:, block:].astype(F32)).astype(BF16)
        tg_ref[at, :] = (acc[at, :] + came[:, :block].astype(F32)).astype(BF16)

    for k in range(1, dp_count):
        slot_copy(k).wait_send()
        ret_copy(k).wait_send()
    for q in range(1, tensor_count):
        cot_copy(q).wait_send()
        part_copy(q).wait_send()


def on_device(dp_count, tensor_count, tok, w, down, up, cot, seq_index, storage):
    resident, rank, block = down.shape
    out_block = up.shape[2]
    rows = tok.shape[0]
    seqs = seq_index.shape[0] // dp_count
    length = rows // seqs
    groups = 2
    wide = block + out_block
    vmem = pl.BlockSpec(memory_space=pltpu.VMEM)
    smem = pl.BlockSpec(memory_space=pltpu.SMEM)
    dma = pltpu.SemaphoreType.DMA
    table, weights = pl.pallas_call(
        functools.partial(routes, dp_count, seqs, resident),
        out_shape=(
            jax.ShapeDtypeStruct((2 * dp_count + seqs,), jnp.int32),
            jax.ShapeDtypeStruct((resident * dp_count + resident,), F32),
        ),
        in_specs=[smem, smem],
        out_specs=(smem, smem),
    )(seq_index, storage)
    return pl.pallas_call(
        functools.partial(kernel, dp_count, tensor_count, groups),
        out_shape=(
            jax.ShapeDtypeStruct((rows, out_block), BF16),
            jax.ShapeDtypeStruct((rows, block), BF16),
            jax.ShapeDtypeStruct((resident, rank, block), F32),
            jax.ShapeDtypeStruct((resident, rank, out_block), F32),
        ),
        in_specs=[smem, smem, vmem, pl.BlockSpec(memory_space=pl.ANY), vmem, vmem, vmem, vmem],
        out_specs=(vmem, vmem, vmem, vmem),
        scratch_shapes=[
            pltpu.VMEM((tensor_count, w.shape[0], out_block), BF16),
            pltpu.VMEM((dp_count * length, wide), BF16),
            pltpu.VMEM((dp_count * length, wide), BF16),
            pltpu.VMEM((dp_count, length, wide), BF16),
            pltpu.VMEM((dp_count, length, wide), BF16),
            pltpu.VMEM((tensor_count, rows, out_block), BF16),
            pltpu.VMEM((tensor_count, rows, out_block), BF16),
            pltpu.VMEM((tensor_count, rows, out_block), BF16),
            pltpu.VMEM((groups, tensor_count, dp_count // groups * length, 2 * rank), BF16),
            pltpu.VMEM((resident, dp_count * length, rank), BF16),
            pltpu.VMEM((resident, dp_count * length, rank), BF16),
            pltpu.VMEM((rows, block), F32),
            dma((tensor_count,)),
            dma((dp_count,)),
            dma((dp_count,)),
            dma((dp_count,)),
            dma((dp_count,)),
            dma((tensor_count,)),
            dma((tensor_count,)),
            dma((tensor_count,)),
            dma((tensor_count,)),
            dma((groups, tensor_count)),
            dma((groups, tensor_count)),
        ],
        compiler_params=pltpu.CompilerParams(
            collective_id=0, has_side_effects=True, vmem_limit_bytes=60 * 1024 * 1024
        ),
    )(
        table, weights, tok.reshape(seqs, length, block), w, down, up, cot,
        cot.reshape(seqs, length, out_block))


def solution(mesh):
    in_specs = (
        P("dp", "tensor"),
        P("tensor", None),
        P("dp", None, "tensor"),
        P("dp", None, "tensor"),
        P("dp", "tensor"),
        P(),
        P(),
    )
    out_specs = (
        P("dp", "tensor"),
        P("dp", "tensor"),
        P("dp", None, "tensor"),
        P("dp", None, "tensor"),
    )
    return jax.shard_map(
        functools.partial(on_device, mesh.shape["dp"], mesh.shape["tensor"]),
        mesh=mesh, in_specs=in_specs, out_specs=out_specs, check_vma=False,
    )
```

```python
import functools

import jax
import jax.numpy as jnp
from jax import lax
from jax.experimental import pallas as pl
from jax.experimental.pallas import tpu as pltpu
from jax.sharding import PartitionSpec as P

adapter_scale = 0.25
MESH = pl.DeviceIdType.MESH
F32 = jnp.float32
BF16 = jnp.bfloat16


def nt_dot(a, b):
    return lax.dot_general(a, b, (((1,), (1,)), ((), ())), preferred_element_type=F32)


def tn_dot(a, b):
    return lax.dot_general(a, b, (((0,), (0,)), ((), ())), preferred_element_type=F32)


def partner(d, k, dp_count):
    out, bit = d, 1
    while bit < dp_count:
        if k & bit:
            out = out + bit - 2 * bit * lax.rem(lax.div(d, jnp.int32(bit)), jnp.int32(2))
        bit *= 2
    return out


def routes(dp_count, seqs, resident, seq_ref, store_ref, table_ref, weight_ref):
    d = lax.axis_index("dp")
    rows = [store_ref[seq_ref[d * seqs + j]] for j in range(seqs)]
    owners = [lax.div(r, jnp.int32(resident)) for r in rows]
    dist = []
    for j in range(seqs):
        slot = jnp.int32(0)
        for k in range(1, dp_count):
            slot = jnp.where(owners[j] == partner(d, k, dp_count), jnp.int32(k), slot)
        dist.append(slot)
    for j in range(seqs):
        table_ref[2 * dp_count + j] = dist[j]
    for k in range(dp_count):
        pick = jnp.int32(0)
        for j in range(seqs):
            pick = jnp.where(dist[j] == k, jnp.int32(j), pick)
        table_ref[k] = pick
    counts = [jnp.float32(0.0)] * resident
    for k in range(dp_count):
        reader = partner(d, k, dp_count)
        found = jnp.int32(-1)
        for j in range(seqs):
            local = store_ref[seq_ref[reader * seqs + j]] - d * resident
            found = jnp.where((local >= 0) & (local < resident), local, found)
        table_ref[dp_count + k] = jnp.maximum(found, 0)
        for a in range(resident):
            hit = jnp.where(found == a, jnp.float32(1.0), jnp.float32(0.0))
            weight_ref[a * dp_count + k] = hit
            counts[a] = counts[a] + hit
    for a in range(resident):
        weight_ref[resident * dp_count + a] = counts[a]


def slot_groups(dp_count):
    order = list(range(dp_count - 1, -1, -1))
    quarter = dp_count // 4
    return [order[:quarter], order[quarter:2 * quarter], order[2 * quarter:]]


def kernel(
    dp_count,
    tensor_count,
    table_ref,
    weight_ref,
    tok_ref,
    w_ref,
    down_hbm,
    up_hbm,
    cot_ref,
    cot_seq_ref,
    kvo_ref,
    tg_ref,
    gd_hbm,
    gu_hbm,
    down_ref,
    up_ref,
    gd_ref,
    gu_ref,
    w_v,
    slot_out,
    slot_in,
    ret_out,
    ret_in,
    cots,
    parts,
    part_in,
    ranks,
    back_m,
    inner_m,
    acc,
    w_sem,
    local_sem,
    slot_ssem,
    slot_rsem,
    ret_ssem,
    ret_rsem,
    cot_ssem,
    cot_rsem,
    part_ssem,
    part_rsem,
    rank_ssem,
    rank_rsem,
):
    d = lax.axis_index("dp")
    t = lax.axis_index("tensor")
    resident, rank, block = down_ref.shape
    out_block = up_ref.shape[2]
    seqs, length = tok_ref.shape[:2]
    rows = seqs * length
    groups = slot_groups(dp_count)
    starts = [sum(len(g) for g in groups[:i]) for i in range(len(groups))]

    def dp_to(k):
        return partner(d, k, dp_count)

    def t_to(q):
        return lax.rem(t + q, tensor_count)

    def t_from(q):
        return lax.rem(t + tensor_count - q, tensor_count)

    def w_copy(i):
        c = t_to(i)
        return pltpu.make_async_copy(
            w_ref.at[:, pl.ds(pl.multiple_of(c * out_block, out_block), out_block)],
            w_v.at[i],
            w_sem.at[i],
        )

    down_copy = pltpu.make_async_copy(down_hbm, down_ref, local_sem.at[0])
    up_copy = pltpu.make_async_copy(up_hbm, up_ref, local_sem.at[1])
    gd_copy = pltpu.make_async_copy(gd_ref, gd_hbm, local_sem.at[2])
    gu_copy = pltpu.make_async_copy(gu_ref, gu_hbm, local_sem.at[3])
    for i in range(tensor_count):
        w_copy(i).start()
    down_copy.start()
    up_copy.start()

    barrier = pltpu.get_barrier_semaphore()
    for k in range(1, dp_count):
        pl.semaphore_signal(barrier, inc=1, device_id={"dp": dp_to(k)}, device_id_type=MESH)
    for q in range(1, tensor_count):
        pl.semaphore_signal(barrier, inc=1, device_id={"tensor": t_to(q)}, device_id_type=MESH)

    for k in range(dp_count):
        pick = table_ref[k]
        target = slot_in if k == 0 else slot_out
        target[k * length:(k + 1) * length, :block] = tok_ref[pick]
        target[k * length:(k + 1) * length, block:] = cot_seq_ref[pick]

    pl.semaphore_wait(barrier, dp_count + tensor_count - 2)

    def cot_copy(q):
        return pltpu.make_async_remote_copy(
            cot_ref, cots.at[q], cot_ssem.at[q], cot_rsem.at[q],
            device_id={"tensor": t_to(q)}, device_id_type=MESH)

    def slot_copy(k):
        at = pl.ds(k * length, length)
        return pltpu.make_async_remote_copy(
            slot_out.at[at], slot_in.at[at], slot_ssem.at[k], slot_rsem.at[k],
            device_id={"dp": dp_to(k)}, device_id_type=MESH)

    def ret_copy(k):
        return pltpu.make_async_remote_copy(
            ret_out.at[k], ret_in.at[k], ret_ssem.at[k], ret_rsem.at[k],
            device_id={"dp": dp_to(k)}, device_id_type=MESH)

    def part_copy(q):
        return pltpu.make_async_remote_copy(
            parts.at[q], part_in.at[q], part_ssem.at[q], part_rsem.at[q],
            device_id={"tensor": t_to(q)}, device_id_type=MESH)

    def rank_rows(g):
        return pl.ds(starts[g] * length, len(groups[g]) * length)

    def rank_copy(g, q):
        return pltpu.make_async_remote_copy(
            ranks.at[t, rank_rows(g)], ranks.at[t, rank_rows(g)], rank_ssem.at[g, q], rank_rsem.at[g, q],
            device_id={"tensor": t_to(q)}, device_id_type=MESH)

    for k in range(dp_count - 1, 0, -1):
        slot_copy(k).start()
    for q in range(1, tensor_count):
        cot_copy(q).start()

    adapter_of = [table_ref[dp_count + k] for k in range(dp_count)]
    weights = [[weight_ref[a * dp_count + k] for k in range(dp_count)] for a in range(resident)]
    counts = [weight_ref[resident * dp_count + a] for a in range(resident)]

    def frozen_block(i, carry):
        w_copy(i).wait()
        parts[i] = jnp.dot(tok_ref[...].reshape(rows, block), w_v[i], preferred_element_type=F32).astype(BF16)
        return carry

    lax.fori_loop(0, tensor_count, frozen_block, 0)

    def rank_stage(g):
        for m, k in enumerate(groups[g]):
            if k:
                slot_copy(k).wait_recv()
            x = slot_in[k * length:(k + 1) * length, :block]
            c = slot_in[k * length:(k + 1) * length, block:]
            inner = nt_dot(x, down_ref[adapter_of[k]])
            back = nt_dot(c, up_ref[adapter_of[k]])
            ranks[t, (starts[g] + m) * length:(starts[g] + m + 1) * length, :] = jnp.concatenate(
                [inner, back], axis=1).astype(BF16)
        for q in range(1, tensor_count):
            rank_copy(g, q).start()

    def base_block(i, carry):
        q = lax.rem(tensor_count - i, tensor_count)
        acc[...] += nt_dot(cots[q], w_v[i])
        return carry

    def use_stage(g):
        for q in range(1, tensor_count):
            s = t_from(q)
            pltpu.make_async_remote_copy(
                ranks.at[s, rank_rows(g)], ranks.at[s, rank_rows(g)], rank_ssem.at[g, q], rank_rsem.at[g, q],
                device_id={"tensor": t_to(q)}, device_id_type=MESH).wait_recv()
        for q in range(1, tensor_count):
            rank_copy(g, q).wait_send()
        total = ranks[0, rank_rows(g)].astype(F32)
        for s in range(1, tensor_count):
            total = total + ranks[s, rank_rows(g)].astype(F32)
        for m, k in enumerate(groups[g]):
            lines = total[m * length:(m + 1) * length]
            inner = lines[:, :rank].astype(BF16)
            back = lines[:, rank:].astype(BF16)
            target = ret_out if k else ret_in
            target[k, :, :block] = (adapter_scale * jnp.dot(
                back, down_ref[adapter_of[k]], preferred_element_type=F32)).astype(BF16)
            target[k, :, block:] = (adapter_scale * jnp.dot(
                inner, up_ref[adapter_of[k]], preferred_element_type=F32)).astype(BF16)
            for a in range(resident):
                at = slice(k * length, (k + 1) * length)
                back_m[a, at, :] = (back.astype(F32) * weights[a][k]).astype(BF16)
                inner_m[a, at, :] = (inner.astype(F32) * weights[a][k]).astype(BF16)
            if k:
                ret_copy(k).start()

    for q in range(1, tensor_count):
        part_copy(q).start()
    half = max(1, tensor_count // 2)
    acc[...] = nt_dot(cot_ref[...], w_v[0])
    for q in range(1, tensor_count):
        cot_copy(q).wait_recv()
    lax.fori_loop(1, half, base_block, 0)
    down_copy.wait()
    up_copy.wait()
    rank_stage(0)
    lax.fori_loop(half, tensor_count, base_block, 0)
    use_stage(0)
    rank_stage(1)
    use_stage(1)
    rank_stage(2)
    use_stage(2)

    x_all = slot_in[:, :block]
    c_all = slot_in[:, block:]
    for a in range(resident):
        gd_ref[a] = tn_dot(back_m[a], x_all) * (
            adapter_scale / jnp.maximum(jnp.full((1, block), counts[a], F32), 1.0))
        gu_ref[a] = tn_dot(inner_m[a], c_all) * (
            adapter_scale / jnp.maximum(jnp.full((1, out_block), counts[a], F32), 1.0))

    gd_copy.start()
    gu_copy.start()
    for q in range(1, tensor_count):
        part_copy(q).wait_recv()
    backbone = parts[0].astype(F32)
    for q in range(1, tensor_count):
        backbone = backbone + part_in[q].astype(F32)
    for k in range(1, dp_count):
        ret_copy(k).wait_recv()
    for j in range(seqs):
        at = slice(j * length, (j + 1) * length)
        came = ret_in[table_ref[2 * dp_count + j]]
        kvo_ref[at, :] = (backbone[at] + came[:, block:].astype(F32)).astype(BF16)
        tg_ref[at, :] = (acc[at, :] + came[:, :block].astype(F32)).astype(BF16)

    for k in range(1, dp_count):
        slot_copy(k).wait_send()
        ret_copy(k).wait_send()
    for q in range(1, tensor_count):
        cot_copy(q).wait_send()
        part_copy(q).wait_send()
    gd_copy.wait()
    gu_copy.wait()


def finish(pieces, *refs):
    n = len(pieces)
    given, out, held = refs[:n], refs[n:2 * n], refs[2 * n:3 * n]
    in_sem, out_sem = refs[3 * n:]
    steps = [(i, p) for i in range(n) for p in range(pieces[i])]

    def move(i, p, source, target, sem, at):
        span = source.shape[0] // pieces[i]
        rows = pl.ds(p * span, span)
        return pltpu.make_async_copy(source.at[rows], target.at[rows], sem.at[at])

    for at, (i, p) in enumerate(steps):
        move(i, p, given[i], held[i], in_sem, at).start()
    for at, (i, p) in enumerate(steps):
        move(i, p, given[i], held[i], in_sem, at).wait()
        move(i, p, held[i], out[i], out_sem, at).start()
    for at, (i, p) in enumerate(steps):
        move(i, p, held[i], out[i], out_sem, at).wait()


def on_device(dp_count, tensor_count, tok, w, down, up, cot, seq_index, storage):
    resident, rank, block = down.shape
    out_block = up.shape[2]
    rows = tok.shape[0]
    seqs = seq_index.shape[0] // dp_count
    length = rows // seqs
    groups = len(slot_groups(dp_count))
    anywhere = pl.BlockSpec(memory_space=pl.ANY)
    wide = block + out_block
    vmem = pl.BlockSpec(memory_space=pltpu.VMEM)
    smem = pl.BlockSpec(memory_space=pltpu.SMEM)
    dma = pltpu.SemaphoreType.DMA
    table, weights = pl.pallas_call(
        functools.partial(routes, dp_count, seqs, resident),
        out_shape=(
            jax.ShapeDtypeStruct((2 * dp_count + seqs,), jnp.int32),
            jax.ShapeDtypeStruct((resident * dp_count + resident,), F32),
        ),
        in_specs=[smem, smem],
        out_specs=(smem, smem),
    )(seq_index, storage)
    results = pl.pallas_call(
        functools.partial(kernel, dp_count, tensor_count),
        out_shape=(
            jax.ShapeDtypeStruct((rows, out_block), BF16),
            jax.ShapeDtypeStruct((rows, block), BF16),
            jax.ShapeDtypeStruct((resident, rank, block), F32),
            jax.ShapeDtypeStruct((resident, rank, out_block), F32),
        ),
        in_specs=[smem, smem, vmem, anywhere, anywhere, anywhere, vmem, vmem],
        out_specs=(vmem, vmem, anywhere, anywhere),
        scratch_shapes=[
            pltpu.VMEM(down.shape, BF16),
            pltpu.VMEM(up.shape, BF16),
            pltpu.VMEM(down.shape, F32),
            pltpu.VMEM(up.shape, F32),
            pltpu.VMEM((tensor_count, w.shape[0], out_block), BF16),
            pltpu.VMEM((dp_count * length, wide), BF16),
            pltpu.VMEM((dp_count * length, wide), BF16),
            pltpu.VMEM((dp_count, length, wide), BF16),
            pltpu.VMEM((dp_count, length, wide), BF16),
            pltpu.VMEM((tensor_count, rows, out_block), BF16),
            pltpu.VMEM((tensor_count, rows, out_block), BF16),
            pltpu.VMEM((tensor_count, rows, out_block), BF16),
            pltpu.VMEM((tensor_count, dp_count * length, 2 * rank), BF16),
            pltpu.VMEM((resident, dp_count * length, rank), BF16),
            pltpu.VMEM((resident, dp_count * length, rank), BF16),
            pltpu.VMEM((rows, block), F32),
            dma((tensor_count,)),
            dma((4,)),
            dma((dp_count,)),
            dma((dp_count,)),
            dma((dp_count,)),
            dma((dp_count,)),
            dma((tensor_count,)),
            dma((tensor_count,)),
            dma((tensor_count,)),
            dma((tensor_count,)),
            dma((groups, tensor_count)),
            dma((groups, tensor_count)),
        ],
        compiler_params=pltpu.CompilerParams(
            collective_id=0, has_side_effects=True, vmem_limit_bytes=60 * 1024 * 1024
        ),
    )(
        table, weights, tok.reshape(seqs, length, block), w, down, up, cot,
        cot.reshape(seqs, length, out_block))
    pieces = (1, 2, resident, 1)
    return pl.pallas_call(
        functools.partial(finish, pieces),
        out_shape=tuple(jax.ShapeDtypeStruct(r.shape, r.dtype) for r in results),
        in_specs=[anywhere] * 4,
        out_specs=(anywhere,) * 4,
        scratch_shapes=[pltpu.VMEM(r.shape, r.dtype) for r in results] + [
            dma((sum(pieces),)), dma((sum(pieces),))],
    )(*results)


def solution(mesh):
    in_specs = (
        P("dp", "tensor"),
        P("tensor", None),
        P("dp", None, "tensor"),
        P("dp", None, "tensor"),
        P("dp", "tensor"),
        P(),
        P(),
    )
    out_specs = (
        P("dp", "tensor"),
        P("dp", "tensor"),
        P("dp", None, "tensor"),
        P("dp", None, "tensor"),
    )
    return jax.shard_map(
        functools.partial(on_device, mesh.shape["dp"], mesh.shape["tensor"]),
        mesh=mesh, in_specs=in_specs, out_specs=out_specs, check_vma=False,
    )
```
